32 devices in a mesh: wide: 8 (over y, x, core), narrow: 4 (over z).
Axes of the slice: x: 2, y: 2, z: 4, core: 2. Of those that a mesh axis runs over, the one named last changes fastest.
Arguments:
- state: float32 [32768, 1, 1024], P(('wide', 'narrow')), may hold values from -6 to 6
- col_blocks: float32 [1, 16, 128, 128], replicated, may hold values from -0.375 to 0.375
- row_blocks: float32 [1, 16, 128, 128], replicated, may hold values from -0.375 to 0.375
- col_pattern: int32 [1, 16], replicated, may hold values from 0 to 63, as said below
- row_pattern: int32 [1, 16], replicated, may hold values from 0 to 63, as said below
- qubit_order: int32 [1, 10], replicated, may hold values from 0 to 9, each once within a row
Outputs:
- amplitudes: float32 [32768, 1, 1024], P(('wide', 'narrow'))
The draws below stay inside these ranges and needn't reach their ends.
Inputs may be any that keep to these rules, and one draw needn't show every extreme that they name: `col_pattern`: each row holds 16 distinct block numbers p; among them are the 8 diagonal blocks p = 9 * b for b = 0 .. 7. `row_pattern`: each row holds 16 distinct block numbers p; among them are the 8 diagonal blocks p = 9 * b for b = 0 .. 7. `qubit_order`: each row is a permutation of 0 to 9.
All inputs are finite; a program needn't handle non-finite values.
Results may differ from the reference program's by a relative error of at most 0.0001.
Values sent between devices are 32-bit elements; how exact they have to be, the bound alone decides.
No kernel may reach another device: no remote copies, remote signals or barrier semaphores. Data moves between devices by JAX's collectives and lax.ppermute only.
A program may use at most 128 MiB of HBM per device.

```python
import jax
import jax.numpy as jnp
from jax import lax

BLK = 128
NB = 8
ROWBITS = 10
NNZ = 16
LAYERS = 1
SLABS = 1
ORDER = 1024
N_WIDE = 8
N_NARROW = 4


def block_pattern(key):

    def one_gate(subkey):
        first_key, second_key = jax.random.split(subkey)
        ranks = jax.random.permutation(first_key, NB * NB - NB)[:NNZ - NB].astype(jnp.int32)
        block_row = ranks // (NB - 1)
        other = ranks % (NB - 1)
        block_col = other + (other >= block_row).astype(jnp.int32)
        offdiag = block_row * NB + block_col
        diagonal = jnp.arange(NB, dtype=jnp.int32) * (NB + 1)
        joined = jnp.concatenate([diagonal, offdiag]).astype(jnp.int32)
        return jax.random.permutation(second_key, joined).astype(jnp.int32)
    return jax.vmap(one_gate)(jax.random.split(key, LAYERS))


def draw_col_pattern(key, part):
    return block_pattern(jax.random.fold_in(key, 101))


def draw_row_pattern(key, part):
    return block_pattern(jax.random.fold_in(key, 202))


def level_of(key, shape, cuts, least, high):
    loudness, own = 1.0, jax.random.fold_in(key, 6)
    for position, blocks in cuts:
        steps = jnp.exp(jax.random.uniform(jax.random.fold_in(own, position), (blocks,), jnp.float32, least / len(cuts), high / len(cuts)))
        loudness = loudness * jnp.repeat(steps, shape[position] // blocks).reshape([-1 if axis == position else 1 for axis in range(len(shape))])
    return loudness


def scatter_about(own_key, extent, deviation, most, pieces=(), kind=jnp.bfloat16):
    array = deviation * jax.random.normal(own_key, extent, jnp.float32)
    if pieces:
        array = array * level_of(own_key, extent, pieces, -0.22, 0.18)
    return jnp.clip(array, -most, most).astype(kind)


def setup_inputs(seed: int = 0) -> dict:
    streams_of = jax.random.split(jax.random.key(seed), 7)
    state = scatter_about(streams_of[0], (N_WIDE * N_NARROW * ORDER, SLABS, ORDER), 1.0, 6.0, ((0, 32),), jnp.float32)
    col_blocks = scatter_about(streams_of[1], (LAYERS, NNZ, BLK, BLK), (2 * BLK) ** -0.5, 0.375, (), jnp.float32)
    row_blocks = scatter_about(streams_of[2], (LAYERS, NNZ, BLK, BLK), (2 * BLK) ** -0.5, 0.375, (), jnp.float32)
    col_pattern = draw_col_pattern(jax.random.fold_in(streams_of[6], 71), 0)
    row_pattern = draw_row_pattern(jax.random.fold_in(streams_of[6], 71), 0)
    qubit_order = jax.vmap(lambda own: jax.random.permutation(own, ROWBITS))(jax.random.split(streams_of[5], LAYERS)).reshape((LAYERS, ROWBITS)).astype(jnp.int32)
    return {"state": state, "col_blocks": col_blocks, "row_blocks": row_blocks, "col_pattern": col_pattern, "row_pattern": row_pattern, "qubit_order": qubit_order}


HIGHEST = lax.Precision.HIGHEST


def column_gate(amplitudes, blocks, pattern):
    block_size = blocks.shape[1]
    groups = amplitudes.shape[-1] // block_size
    leading = amplitudes.shape[:-1]
    grouped = amplitudes.reshape(leading + (groups, block_size))
    picked = jnp.take(grouped, (pattern % groups).astype(jnp.int32), axis=-2)
    blended = jnp.einsum("...ke,kde->...kd", picked, blocks, precision=HIGHEST)
    placer = ((pattern[:, None] // groups) == jnp.arange(groups, dtype=jnp.int32)[None, :]).astype(jnp.float32)
    placed = jnp.einsum("...kd,kb->...bd", blended, placer, precision=HIGHEST)
    return placed.reshape(amplitudes.shape)


def row_gate(amplitudes, blocks, pattern):
    block_size = blocks.shape[1]
    groups = amplitudes.shape[0] // block_size
    grouped = amplitudes.reshape(groups, block_size, -1)
    picked = jnp.take(grouped, (pattern % groups).astype(jnp.int32), axis=0)
    blended = jnp.einsum("kde,kem->kdm", blocks, picked, precision=HIGHEST)
    placer = ((pattern[:, None] // groups) == jnp.arange(groups, dtype=jnp.int32)[None, :]).astype(jnp.float32)
    placed = jnp.einsum("kb,kdm->bdm", placer, blended, precision=HIGHEST)
    return placed.reshape(amplitudes.shape)


def relabel_source(ordering, row_total):
    positions = jnp.arange(row_total, dtype=jnp.int32)
    qubits = jnp.arange(ordering.shape[0], dtype=jnp.int32)
    digits = (positions[:, None] >> qubits[None, :]) & 1
    return jnp.sum(digits << ordering[None, :].astype(jnp.int32), axis=1).astype(jnp.int32)


def reference(state, col_blocks, row_blocks, col_pattern, row_pattern, qubit_order):
    wide_bits = N_WIDE.bit_length() - 1
    devices_all = N_WIDE * N_NARROW
    current = state.reshape(devices_all, ORDER, SLABS, ORDER)
    for layer_index in range(LAYERS):
        rblocks = row_blocks[layer_index]
        rpattern = row_pattern[layer_index]
        current = lax.map(lambda shard: row_gate(shard, rblocks, rpattern), current)
        source = relabel_source(qubit_order[layer_index], ORDER)
        current = jnp.take(current, source, axis=1)
        qubit = wide_bits - 1 - layer_index
        shaped = current.reshape(N_WIDE >> (qubit + 1), 2, (1 << qubit) * N_NARROW, 2, ORDER // 2, SLABS, ORDER)
        current = jnp.swapaxes(shaped, 1, 3).reshape(devices_all, ORDER, SLABS, ORDER)
        if layer_index + 1 < LAYERS:
            cblocks = col_blocks[layer_index]
            cpattern = col_pattern[layer_index]
            current = lax.map(lambda shard: column_gate(shard, cblocks, cpattern), current)
    shaped = current.reshape(N_WIDE, N_NARROW, N_NARROW, ORDER // N_NARROW, SLABS, ORDER)
    current = jnp.swapaxes(shaped, 1, 2).reshape(devices_all, ORDER, SLABS, ORDER)
    fblocks = col_blocks[LAYERS - 1]
    fpattern = col_pattern[LAYERS - 1]
    current = lax.map(lambda shard: column_gate(shard, fblocks, fpattern), current)
    return current.reshape(devices_all * ORDER, SLABS, ORDER)
```

```python
import functools

import jax
import jax.numpy as jnp
from jax import lax
from jax.experimental import pallas as pl
from jax.experimental.pallas import tpu as pltpu
from jax.sharding import PartitionSpec as P


F32, BF16, I32 = jnp.float32, jnp.bfloat16, jnp.int32


SHARES = (1, 2, 4, 5, 4)

BULK = pl.BlockSpec(memory_space=pltpu.HBM)
VECTORS = pl.BlockSpec(memory_space=pltpu.VMEM)
VMEM_BYTES = 67_043_328


def split(value):
    high = value.astype(BF16)
    return high, (value - high.astype(F32)).astype(BF16)


def dot3(lhs, rhs_high, rhs_low, contract):
    dot = functools.partial(
        lax.dot_general, dimension_numbers=(contract, ((), ())), preferred_element_type=F32
    )
    lines = lhs.shape[0] // 2
    both = dot(lhs, rhs_high)
    return both[:lines] + (both[lines:] + dot(lhs[:lines], rhs_low))


def aligned(index, size):
    return pl.ds(pl.multiple_of(index * size, size), size)


def load_gates(row_pattern, col_pattern, row_copy, col_copy, state_hbm, dense, col_gate, state, columns, row_blocks, col_blocks, sems):
    groups, _, block = columns.shape
    nnz = row_blocks.shape[0]
    state_copies = []
    for c in range(groups):
        copy = pltpu.make_async_copy(state_hbm.at[:, c, :], columns.at[c], sems.at[c])
        copy.start()
        state_copies.append(copy)
    dense[...] = jnp.zeros_like(dense)
    for half in col_gate:
        half[...] = jnp.zeros_like(half)
    for copy in row_copy:
        copy.wait()
    for k in range(nnz):
        p = row_pattern[0, k]
        first = (p // groups) * (block * groups) + p % groups
        dense[pl.ds(first, block, stride=groups), :] = row_blocks[k]
    for copy in col_copy:
        copy.wait()
    for k in range(nnz):
        p = col_pattern[0, k]
        for half, value in zip(col_gate, split(col_blocks[k])):
            half[aligned(p // groups, block), aligned(p % groups, block)] = value
    for c in range(groups):
        state_copies[c].wait()
        for half, value in zip(state, split(columns[c])):
            half[:, c * block : (c + 1) * block] = value


def apply_gates(low0, count, order, dense, col_gate, state, gathered, gate, rowed, keep_ref, send_ref):
    rows, width = state[0].shape
    groups = dense.shape[0] // rows
    block = width // groups
    row_bits = rows.bit_length() - 1
    narrow_bits = lax.axis_size("narrow").bit_length() - 1
    wide_bits = lax.axis_size("wide").bit_length() - 1
    pieces = 1 << narrow_bits
    half = pieces // 2
    lines = pieces * count
    own_side = lax.axis_index("wide") >> (wide_bits - 1)
    own_low = lax.axis_index("narrow") & (half - 1)

    def source(row):
        total = 0
        for j in range(row_bits):
            total = total + (((row >> j) & 1) << order[0, j])
        return total

    lows = [source(jnp.int32(low)) for low in range(8)]
    for i in range(pieces):
        side = own_side if i < half else 1 - own_side
        piece = side * half + ((i % half) ^ own_low)
        base = piece * (rows // pieces) + low0

        def move(g, carry, i=i, base=base):
            start = source(base + g * 8)
            for low in range(8):
                to = i * count + g * 8 + low
                gathered[aligned(to, groups), :] = dense[aligned(start + lows[low], groups), :]
            return carry

        lax.fori_loop(0, count // 8, move, 0)
    for c in range(groups):
        values = split(gathered[pl.ds(c, lines, stride=groups), :])
        for s in range(2):
            gate[s * lines : (s + 1) * lines, c * block : (c + 1) * block] = values[s]

    tile = 2 * block

    def rows_step(n, carry):
        at = aligned(n, tile)
        values = split(dot3(gate[...], state[0][:, at], state[1][:, at], ((1,), (0,))))
        for s in range(2):
            rowed[s * lines : (s + 1) * lines, at] = values[s]
        return carry

    lax.fori_loop(0, width // tile, rows_step, 0)

    def cols_step(n, carry):
        at = aligned(n, tile)
        value = dot3(rowed[...], col_gate[0][at, :], col_gate[1][at, :], ((1,), (1,)))
        for c in range(2):
            part = value[:, c * block : (c + 1) * block]
            keep_ref[pl.ds(n * 2 + c, half * count, stride=groups), :] = part[: half * count]
            send_ref[pl.ds(n * 2 + c, half * count, stride=groups), :] = part[half * count :]
        return carry

    lax.fori_loop(0, width // tile, cols_step, 0)


def first_kernel(low0, count, row_pattern_hbm, col_pattern_hbm, order_hbm, state_hbm, row_hbm, col_hbm,
                 keep_ref, send_ref, dense, col_high, col_low, state_high, state_low,
                 columns, row_blocks, col_blocks, row_pattern, col_pattern, order, gathered, gate, rowed, sems):
    groups = columns.shape[0]
    copies = [
        pltpu.make_async_copy(source, target, sems.at[groups + i])
        for i, (source, target) in enumerate((
            (row_pattern_hbm, row_pattern), (row_hbm, row_blocks), (col_pattern_hbm, col_pattern),
            (col_hbm, col_blocks), (order_hbm, order)))
    ]
    for copy in copies:
        copy.start()
    load_gates(row_pattern, col_pattern, copies[:2], copies[2:4], state_hbm, dense, (col_high, col_low),
               (state_high, state_low), columns, row_blocks, col_blocks, sems)
    copies[4].wait()
    apply_gates(low0, count, order, dense, (col_high, col_low), (state_high, state_low), gathered,
                gate, rowed, keep_ref, send_ref)


def next_kernel(low0, count, order_hbm, dense, col_high, col_low, state_high, state_low,
                keep_ref, send_ref, order, gathered, gate, rowed, sem):
    copy = pltpu.make_async_copy(order_hbm, order, sem)
    copy.start()
    copy.wait()
    apply_gates(low0, count, order, dense, (col_high, col_low), (state_high, state_low), gathered,
                gate, rowed, keep_ref, send_ref)


def chunk_scratch(order, lines, groups, block):
    both = pltpu.VMEM((2 * lines, groups * block), BF16)
    return [pltpu.SMEM(order.shape, I32), pltpu.VMEM((lines * groups, block), F32), both, both]


def first_chunk(low0, count, pieces, state, row_blocks, col_blocks, row_pattern, col_pattern, order):
    rows, groups, block = state.shape
    width = groups * block
    lines = pieces * count
    part = pltpu.VMEM((lines // 2 * groups, block), F32)
    held = 4 * width * (2 * rows + width + lines) + (16 << 10)
    return pl.pallas_call(
        functools.partial(first_kernel, low0, count),
        out_shape=(part, part, pltpu.VMEM((rows * groups, block), F32),
                   pltpu.VMEM((width, width), BF16), pltpu.VMEM((width, width), BF16),
                   pltpu.VMEM((rows, width), BF16), pltpu.VMEM((rows, width), BF16)),
        in_specs=[BULK] * 6,
        out_specs=(VECTORS,) * 7,
        scratch_shapes=[
            pltpu.VMEM((groups, rows, block), F32),
            pltpu.VMEM(row_blocks.shape, F32),
            pltpu.VMEM(col_blocks.shape, F32),
            pltpu.SMEM(row_pattern.shape, I32),
            pltpu.SMEM(col_pattern.shape, I32),
            *chunk_scratch(order, lines, groups, block),
            pltpu.SemaphoreType.DMA((groups + 5,)),
        ],
        compiler_params=pltpu.CompilerParams(vmem_limit_bytes=VMEM_BYTES - held),
        name="first_gates",
    )(row_pattern, col_pattern, order, state, row_blocks, col_blocks)


def next_chunk(low0, count, pieces, order, prepared):
    _, width = prepared[-1].shape
    block = prepared[0].shape[1]
    groups = width // block
    lines = pieces * count
    part = pltpu.VMEM((lines // 2 * groups, block), F32)
    return pl.pallas_call(
        functools.partial(next_kernel, low0, count),
        out_shape=(part, part),
        in_specs=[BULK] + [VECTORS] * 5,
        out_specs=(VECTORS,) * 2,
        scratch_shapes=[*chunk_scratch(order, lines, groups, block), pltpu.SemaphoreType.DMA],
        compiler_params=pltpu.CompilerParams(vmem_limit_bytes=16 << 20),
    )(order, *prepared)


def pick_kernel(keep, swapped, *outs):
    wide, narrow = lax.axis_size("wide"), lax.axis_size("narrow")
    half = narrow // 2
    side = lax.axis_index("wide") // (wide // 2)
    high = lax.axis_index("narrow") // half
    for step, out in enumerate(outs):
        stay = (high ^ (step // half)) == side

        @pl.when(stay)
        def _(out=out, step=step):
            out[...] = keep[step % half]

        @pl.when(jnp.logical_not(stay))
        def _(out=out, step=step):
            out[...] = swapped[step % half]


def pick_chunk(keep, swapped, steps):
    return pl.pallas_call(
        pick_kernel,
        out_shape=(pltpu.VMEM(keep.shape[1:], F32),) * steps,
        in_specs=[VECTORS] * 2,
        out_specs=(VECTORS,) * steps,
        compiler_params=pltpu.CompilerParams(vmem_limit_bytes=2 << 20),
    )(keep, swapped)


def place_kernel(low0, count, *refs):
    steps = lax.axis_size("narrow")
    pieces, result, sems = refs[:steps], refs[-2], refs[-1]
    place = lax.axis_index("narrow")
    copies = []
    for step in range(steps):
        copy = pltpu.make_async_copy(pieces[step], result.at[place ^ step, pl.ds(low0, count)], sems.at[step])
        copy.start()
        copies.append(copy)
    for copy in copies:
        copy.wait()


def place_chunk(low0, count, pieces, shape, result):
    extra = [] if result is None else [result]
    return pl.pallas_call(
        functools.partial(place_kernel, low0, count),
        out_shape=jax.ShapeDtypeStruct(shape, F32),
        in_specs=[VECTORS] * len(pieces) + [BULK] * len(extra),
        out_specs=BULK,
        scratch_shapes=[pltpu.SemaphoreType.DMA((len(pieces),))],
        input_output_aliases={len(pieces): 0} if extra else {},
        compiler_params=pltpu.CompilerParams(vmem_limit_bytes=2 << 20),
    )(*pieces, *extra)


def local(state, col_blocks, row_blocks, col_pattern, row_pattern, qubit_order):
    rows, slabs, width = state.shape
    block = row_blocks.shape[-1]
    groups = slabs * width // block
    wide, narrow = lax.axis_size("wide"), lax.axis_size("narrow")
    top = wide // 2
    half = narrow // 2
    per_piece = rows // narrow
    unit = per_piece // sum(SHARES)
    wide_pairs = [(w, w ^ top) for w in range(wide)]
    counts = [share * unit for share in SHARES]
    lows = [sum(counts[:j]) for j in range(len(counts))]
    parts = []
    prepared = None
    for j, count in enumerate(counts):
        if j == 0:
            keep, send, *prepared = first_chunk(
                lows[0], count, narrow, state.reshape(rows, groups, block), row_blocks[0],
                col_blocks[0], row_pattern, col_pattern, qubit_order)
        else:
            keep, send = next_chunk(lows[j], count, narrow, qubit_order, prepared)
        shape = (half, count, groups, block)
        swapped = lax.ppermute(send.reshape(shape), "wide", wide_pairs)
        picked = pick_chunk(keep.reshape(shape), swapped, narrow)
        parts.append(picked[:1] + tuple(
            lax.ppermute(picked[step], "narrow", [(n, n ^ step) for n in range(narrow)])
            for step in range(1, narrow)))
    result = None
    for j, count in enumerate(counts):
        result = place_chunk(lows[j], count, parts[j], (narrow, per_piece, groups, block), result)
    return result.reshape(state.shape)


def solution(mesh):
    return jax.shard_map(
        local,
        mesh=mesh,
        in_specs=(P(("wide", "narrow"), None, None), P(), P(), P(), P(), P()),
        out_specs=P(("wide", "narrow"), None, None),
        check_vma=False,
    )
```

```python
import functools

import jax
import jax.numpy as jnp
from jax import lax
from jax.experimental import pallas as pl
from jax.experimental.pallas import tpu as pltpu
from jax.sharding import PartitionSpec as P


F32, BF16, I32 = jnp.float32, jnp.bfloat16, jnp.int32


SHARES = (1, 2, 3, 4, 6, 8, 8)
FIRST = 3

BULK = pl.BlockSpec(memory_space=pltpu.HBM)
VECTORS = pl.BlockSpec(memory_space=pltpu.VMEM)
VMEM_BYTES = 67_043_328
SLACK = 1 << 19


def split(value):
    high = value.astype(BF16)
    return high, (value - high.astype(F32)).astype(BF16)


def dot3(lhs, rhs_high, rhs_low, contract):
    dot = functools.partial(
        lax.dot_general, dimension_numbers=(contract, ((), ())), preferred_element_type=F32
    )
    lines = lhs.shape[0] // 2
    both = dot(lhs, rhs_high)
    return both[:lines] + (both[lines:] + dot(lhs[:lines], rhs_low))


def aligned(index, size):
    return pl.ds(pl.multiple_of(index * size, size), size)


def pick_rows(chunks, order, dense, gathered, gate):
    lines, width = gate.shape[0] // 2, gate.shape[1]
    block = gathered.shape[1]
    groups = width // block
    rows = dense.shape[0] // groups
    narrow = lax.axis_size("narrow")
    half = narrow // 2
    own_side = lax.axis_index("wide") // (lax.axis_size("wide") // 2)
    own_low = lax.axis_index("narrow") & (half - 1)

    def source(row):
        total = 0
        for j in range(rows.bit_length() - 1):
            total = total + (((row >> j) & 1) << order[0, j])
        return total

    lows = [source(jnp.int32(low)) for low in range(8)]
    line = 0
    for low0, count in chunks:
        for i in range(narrow):
            side = own_side if i < half else 1 - own_side
            piece = side * half + ((i % half) ^ own_low)
            base = piece * (rows // narrow) + low0

            def move(g, carry, line=line, base=base):
                start = source(base + g * 8)
                for low in range(8):
                    to = line + g * 8 + low
                    gathered[aligned(to, groups), :] = dense[aligned(start + lows[low], groups), :]
                return carry

            lax.fori_loop(0, count // 8, move, 0)
            line += count
    for c in range(groups):
        values = split(gathered[pl.ds(c, lines, stride=groups), :])
        for s in range(2):
            gate[s * lines : (s + 1) * lines, c * block : (c + 1) * block] = values[s]


def stacked(value):
    return jnp.concatenate(split(value), axis=0)


def store(value, outs):
    line = 0
    for ref in outs:
        block = ref.shape[1]
        groups = value.shape[1] // block
        lines = ref.shape[0] // groups
        for c in range(groups):
            ref[pl.ds(c, lines, stride=groups), :] = value[line : line + lines, c * block : (c + 1) * block]
        line += lines


def first_kernel(chunks, row_pattern_hbm, col_pattern_hbm, order_hbm, state_hbm, row_hbm, col_hbm, *refs):
    parts = 2 * len(chunks)
    outs, refs = refs[:parts], refs[parts:]
    (dense, col_high, col_low, state_high, state_low,
     columns, row_blocks, col_blocks, row_pattern, col_pattern, order, gathered, gate, sems) = refs
    groups, _, block = columns.shape
    nnz = row_blocks.shape[0]
    state_copies = [
        pltpu.make_async_copy(state_hbm.at[:, c, :], columns.at[c], sems.at[c]) for c in range(groups)
    ]
    order_copy, row_pattern_copy, col_pattern_copy, row_copy, col_copy = [
        pltpu.make_async_copy(source, target, sems.at[groups + i])
        for i, (source, target) in enumerate((
            (order_hbm, order), (row_pattern_hbm, row_pattern), (col_pattern_hbm, col_pattern),
            (row_hbm, row_blocks), (col_hbm, col_blocks)))
    ]
    for copy in (order_copy, row_pattern_copy, col_pattern_copy, row_copy, col_copy, *state_copies):
        copy.start()
    dense[...] = jnp.zeros_like(dense)
    for half in (col_high, col_low):
        half[...] = jnp.zeros_like(half)
    row_pattern_copy.wait()
    order_copy.wait()
    col_pattern_copy.wait()
    row_copy.wait()
    for k in range(nnz):
        p = row_pattern[0, k]
        first = (p // groups) * (block * groups) + p % groups
        dense[pl.ds(first, block, stride=groups), :] = row_blocks[k]
    pick_rows(chunks, order, dense, gathered, gate)
    col_copy.wait()
    for k in range(nnz):
        p = col_pattern[0, k]
        for half, value in zip((col_high, col_low), split(col_blocks[k])):
            half[aligned(p // groups, block), aligned(p % groups, block)] = value
    for c in range(groups):
        state_copies[c].wait()
        for half, value in zip((state_high, state_low), split(columns[c])):
            half[:, c * block : (c + 1) * block] = value
    store(both_gates(gate, state_high, state_low, col_high, col_low), outs)


def both_gates(gate, state_high, state_low, col_high, col_low):
    rowed = dot3(gate[...], state_high[...], state_low[...], ((1,), (0,)))
    return dot3(stacked(rowed), col_high[...], col_low[...], ((1,), (1,)))


def next_kernel(chunks, order_hbm, dense, col_high, col_low, state_high, state_low, *refs):
    parts = 2 * len(chunks)
    outs, (order, gathered, gate, sem) = refs[:parts], refs[parts:]
    copy = pltpu.make_async_copy(order_hbm, order, sem)
    copy.start()
    copy.wait()
    pick_rows(chunks, order, dense, gathered, gate)
    store(both_gates(gate, state_high, state_low, col_high, col_low), outs)


def chunk_shapes(chunks, narrow, groups, block):
    shapes = []
    for _, count in chunks:
        shapes += [pltpu.VMEM((narrow // 2 * count * groups, block), F32)] * 2
    return shapes


def chunk_scratch(chunks, narrow, order, groups, block):
    lines = narrow * sum(chunk[1] for chunk in chunks)
    return [
        pltpu.SMEM(order.shape, I32),
        pltpu.VMEM((lines * groups, block), F32),
        pltpu.VMEM((2 * lines, groups * block), BF16),
    ]


def first_chunks(chunks, narrow, state, row_blocks, col_blocks, row_pattern, col_pattern, order):
    rows, groups, block = state.shape
    width = groups * block
    parts = chunk_shapes(chunks, narrow, groups, block)
    held = 4 * width * (2 * rows + width) + sum(4 * part.shape[0] * block for part in parts) + SLACK
    return pl.pallas_call(
        functools.partial(first_kernel, chunks),
        out_shape=(*parts, pltpu.VMEM((rows * groups, block), F32),
                   pltpu.VMEM((width, width), BF16), pltpu.VMEM((width, width), BF16),
                   pltpu.VMEM((rows, width), BF16), pltpu.VMEM((rows, width), BF16)),
        in_specs=[BULK] * 6,
        out_specs=(VECTORS,) * (len(parts) + 5),
        scratch_shapes=[
            pltpu.VMEM((groups, rows, block), F32),
            pltpu.VMEM(row_blocks.shape, F32),
            pltpu.VMEM(col_blocks.shape, F32),
            pltpu.SMEM(row_pattern.shape, I32),
            pltpu.SMEM(col_pattern.shape, I32),
            *chunk_scratch(chunks, narrow, order, groups, block),
            pltpu.SemaphoreType.DMA((groups + 5,)),
        ],
        compiler_params=pltpu.CompilerParams(vmem_limit_bytes=VMEM_BYTES - held),
        name="first_gates",
    )(row_pattern, col_pattern, order, state, row_blocks, col_blocks)


def next_chunks(chunks, narrow, order, prepared):
    _, width = prepared[-1].shape
    block = prepared[0].shape[1]
    groups = width // block
    parts = chunk_shapes(chunks, narrow, groups, block)
    return pl.pallas_call(
        functools.partial(next_kernel, chunks),
        out_shape=tuple(parts),
        in_specs=[BULK] + [VECTORS] * 5,
        out_specs=(VECTORS,) * len(parts),
        scratch_shapes=[*chunk_scratch(chunks, narrow, order, groups, block), pltpu.SemaphoreType.DMA],
        compiler_params=pltpu.CompilerParams(vmem_limit_bytes=24 << 20),
    )(order, *prepared)


def pick_kernel(keep, swapped, *outs):
    wide, narrow = lax.axis_size("wide"), lax.axis_size("narrow")
    half = narrow // 2
    side = lax.axis_index("wide") // (wide // 2)
    high = lax.axis_index("narrow") // half
    for step, out in enumerate(outs):
        stay = (high ^ (step // half)) == side

        @pl.when(stay)
        def _(out=out, step=step):
            out[...] = keep[step % half]

        @pl.when(jnp.logical_not(stay))
        def _(out=out, step=step):
            out[...] = swapped[step % half]


def pick_chunk(keep, swapped, steps):
    return pl.pallas_call(
        pick_kernel,
        out_shape=(pltpu.VMEM(keep.shape[1:], F32),) * steps,
        in_specs=[VECTORS] * 2,
        out_specs=(VECTORS,) * steps,
        compiler_params=pltpu.CompilerParams(vmem_limit_bytes=2 << 20),
    )(keep, swapped)


def place_kernel(low0, count, *refs):
    steps = lax.axis_size("narrow")
    pieces, result, sems = refs[:steps], refs[-2], refs[-1]
    place = lax.axis_index("narrow")
    copies = []
    for step in range(steps):
        copy = pltpu.make_async_copy(pieces[step], result.at[place ^ step, pl.ds(low0, count)], sems.at[step])
        copy.start()
        copies.append(copy)
    for copy in copies:
        copy.wait()


def place_chunk(chunk, pieces, shape, result):
    low0, count = chunk
    extra = [] if result is None else [result]
    return pl.pallas_call(
        functools.partial(place_kernel, low0, count),
        out_shape=jax.ShapeDtypeStruct(shape, F32),
        in_specs=[VECTORS] * len(pieces) + [BULK] * len(extra),
        out_specs=BULK,
        scratch_shapes=[pltpu.SemaphoreType.DMA((len(pieces),))],
        input_output_aliases={len(pieces): 0} if extra else {},
        compiler_params=pltpu.CompilerParams(vmem_limit_bytes=2 << 20),
    )(*pieces, *extra)


def local(state, col_blocks, row_blocks, col_pattern, row_pattern, qubit_order):
    rows, slabs, width = state.shape
    block = row_blocks.shape[-1]
    groups = slabs * width // block
    wide, narrow = lax.axis_size("wide"), lax.axis_size("narrow")
    top = wide // 2
    half = narrow // 2
    per_piece = rows // narrow
    unit = per_piece // sum(SHARES)
    wide_pairs = [(w, w ^ top) for w in range(wide)]
    counts = [share * unit for share in SHARES]
    chunks = [(sum(counts[:j]), count) for j, count in enumerate(counts)]
    parts = []
    made = first_chunks(
        chunks[:FIRST], narrow, state.reshape(rows, groups, block), row_blocks[0], col_blocks[0],
        row_pattern, col_pattern, qubit_order)
    sides = list(made[: 2 * FIRST])
    prepared = made[len(sides) :]
    for j, chunk in enumerate(chunks):
        _, count = chunk
        if j >= FIRST:
            sides += next_chunks((chunk,), narrow, qubit_order, prepared)
        keep, send = sides.pop(0), sides.pop(0)
        shape = (half, count, groups, block)
        swapped = lax.ppermute(send.reshape(shape), "wide", wide_pairs)
        picked = pick_chunk(keep.reshape(shape), swapped, narrow)
        moved = [picked[0]]
        for step in range(1, narrow):
            moved.append(lax.ppermute(picked[step], "narrow", [(n, n ^ step) for n in range(narrow)]))
        parts.append(tuple(moved))
    result = None
    for j, chunk in enumerate(chunks):
        result = place_chunk(chunk, parts[j], (narrow, per_piece, groups, block), result)
    return result.reshape(state.shape)


def solution(mesh):
    return jax.shard_map(
        local,
        mesh=mesh,
        in_specs=(P(("wide", "narrow"), None, None), P(), P(), P(), P(), P()),
        out_specs=P(("wide", "narrow"), None, None),
        check_vma=False,
    )
```

```python
import functools

import jax
import jax.numpy as jnp
from jax import lax
from jax.experimental import pallas as pl
from jax.experimental.pallas import tpu as pltpu
from jax.sharding import PartitionSpec as P


F32, BF16, I32 = jnp.float32, jnp.bfloat16, jnp.int32


SHARES = (2, 2, 3, 4, 6, 8, 7)
FIRST = 3

BULK = pl.BlockSpec(memory_space=pltpu.HBM)
VECTORS = pl.BlockSpec(memory_space=pltpu.VMEM)
VMEM_BYTES = 67_043_328
SLACK = 1 << 19


def split(value):
    high = value.astype(BF16)
    return high, (value - high.astype(F32)).astype(BF16)


def dot3(lhs, rhs_high, rhs_low, contract):
    dot = functools.partial(
        lax.dot_general, dimension_numbers=(contract, ((), ())), preferred_element_type=F32
    )
    lines = lhs.shape[0] // 2
    both = dot(lhs, rhs_high)
    return both[:lines] + (both[lines:] + dot(lhs[:lines], rhs_low))


def aligned(index, size):
    return pl.ds(pl.multiple_of(index * size, size), size)


def pick_rows(chunks, order, dense, gathered, gate):
    lines, width = gate.shape[0] // 2, gate.shape[1]
    block = gathered.shape[1]
    groups = width // block
    rows = dense.shape[0] // groups
    narrow = lax.axis_size("narrow")
    half = narrow // 2
    own_side = lax.axis_index("wide") // (lax.axis_size("wide") // 2)
    own_low = lax.axis_index("narrow") & (half - 1)

    leads = [groups << order[0, j] for j in range(rows.bit_length() - 1)]

    def source(row):
        return sum(lead for j, lead in enumerate(leads) if row >> j & 1)

    per_piece = rows // narrow
    high_leads = leads[per_piece.bit_length() - 1 :]
    lows = [source(low) for low in range(8)]
    line = 0
    for low0, count in chunks:
        for i in range(narrow):
            side = own_side if i < half else 1 - own_side
            piece = side * half + ((i % half) ^ own_low)
            base = sum((piece >> b & 1) * lead for b, lead in enumerate(high_leads))
            for g in range(low0, low0 + count, 8):
                start = base + source(g)
                for low in range(8):
                    at = pl.ds(pl.multiple_of(start + lows[low], groups), groups)
                    gathered[line * groups : (line + 1) * groups, :] = dense[at, :]
                    line += 1
    for c in range(groups):
        values = split(gathered[pl.ds(c, lines, stride=groups), :])
        for s in range(2):
            gate[s * lines : (s + 1) * lines, c * block : (c + 1) * block] = values[s]


def stacked(value):
    return jnp.concatenate(split(value), axis=0)


def store(value, outs):
    line = 0
    for ref in outs:
        block = ref.shape[1]
        groups = value.shape[1] // block
        lines = ref.shape[0] // groups
        for c in range(groups):
            ref[pl.ds(c, lines, stride=groups), :] = value[line : line + lines, c * block : (c + 1) * block]
        line += lines


def first_kernel(chunks, row_pattern_hbm, col_pattern_hbm, order_hbm, state_hbm, row_hbm, col_hbm, *refs):
    parts = 2 * len(chunks)
    outs, refs = refs[:parts], refs[parts:]
    (dense, col_high, col_low, state_high, state_low,
     columns, row_blocks, col_blocks, row_pattern, col_pattern, order, gathered, gate, sems) = refs
    groups, _, block = columns.shape
    nnz = row_blocks.shape[0]
    state_copies = [
        pltpu.make_async_copy(state_hbm.at[:, c, :], columns.at[c], sems.at[c]) for c in range(groups)
    ]
    order_copy, row_pattern_copy, col_pattern_copy, row_copy, col_copy = [
        pltpu.make_async_copy(source, target, sems.at[groups + i])
        for i, (source, target) in enumerate((
            (order_hbm, order), (row_pattern_hbm, row_pattern), (col_pattern_hbm, col_pattern),
            (row_hbm, row_blocks), (col_hbm, col_blocks)))
    ]
    for copy in (order_copy, row_pattern_copy, col_pattern_copy, row_copy, col_copy, *state_copies):
        copy.start()
    dense[...] = jnp.zeros_like(dense)
    for half in (col_high, col_low):
        half[...] = jnp.zeros_like(half)
    row_pattern_copy.wait()
    order_copy.wait()
    col_pattern_copy.wait()
    row_copy.wait()
    for k in range(nnz):
        p = row_pattern[0, k]
        first = (p // groups) * (block * groups) + p % groups
        dense[pl.ds(first, block, stride=groups), :] = row_blocks[k]
    pick_rows(chunks, order, dense, gathered, gate)
    col_copy.wait()
    for k in range(nnz):
        p = col_pattern[0, k]
        for half, value in zip((col_high, col_low), split(col_blocks[k])):
            half[aligned(p // groups, block), aligned(p % groups, block)] = value
    for c in range(groups):
        if c % 4 == 0:
            for copy in state_copies[c : c + 4]:
                copy.wait()
        for half, value in zip((state_high, state_low), split(columns[c])):
            half[:, c * block : (c + 1) * block] = value
    store(both_gates(gate, state_high, state_low, col_high, col_low), outs)


def both_gates(gate, state_high, state_low, col_high, col_low):
    rowed = dot3(gate[...], state_high[...], state_low[...], ((1,), (0,)))
    return dot3(stacked(rowed), col_high[...], col_low[...], ((1,), (1,)))


def next_kernel(chunks, order_hbm, dense, col_high, col_low, state_high, state_low, *refs):
    parts = 2 * len(chunks)
    outs, (order, gathered, gate, sem) = refs[:parts], refs[parts:]
    copy = pltpu.make_async_copy(order_hbm, order, sem)
    copy.start()
    copy.wait()
    pick_rows(chunks, order, dense, gathered, gate)
    store(both_gates(gate, state_high, state_low, col_high, col_low), outs)


def chunk_shapes(chunks, narrow, groups, block):
    shapes = []
    for _, count in chunks:
        shapes += [pltpu.VMEM((narrow // 2 * count * groups, block), F32)] * 2
    return shapes


def chunk_scratch(chunks, narrow, order, groups, block):
    lines = narrow * sum(chunk[1] for chunk in chunks)
    return [
        pltpu.SMEM(order.shape, I32),
        pltpu.VMEM((lines * groups, block), F32),
        pltpu.VMEM((2 * lines, groups * block), BF16),
    ]


def first_chunks(chunks, narrow, state, row_blocks, col_blocks, row_pattern, col_pattern, order):
    rows, groups, block = state.shape
    width = groups * block
    parts = chunk_shapes(chunks, narrow, groups, block)
    held = 4 * width * (2 * rows + width) + sum(4 * part.shape[0] * block for part in parts) + SLACK
    return pl.pallas_call(
        functools.partial(first_kernel, chunks),
        out_shape=(*parts, pltpu.VMEM((rows * groups, block), F32),
                   pltpu.VMEM((width, width), BF16), pltpu.VMEM((width, width), BF16),
                   pltpu.VMEM((rows, width), BF16), pltpu.VMEM((rows, width), BF16)),
        in_specs=[BULK] * 6,
        out_specs=(VECTORS,) * (len(parts) + 5),
        scratch_shapes=[
            pltpu.VMEM((groups, rows, block), F32),
            pltpu.VMEM(row_blocks.shape, F32),
            pltpu.VMEM(col_blocks.shape, F32),
            pltpu.SMEM(row_pattern.shape, I32),
            pltpu.SMEM(col_pattern.shape, I32),
            *chunk_scratch(chunks, narrow, order, groups, block),
            pltpu.SemaphoreType.DMA((groups + 5,)),
        ],
        compiler_params=pltpu.CompilerParams(vmem_limit_bytes=VMEM_BYTES - held),
        name="first_gates",
    )(row_pattern, col_pattern, order, state, row_blocks, col_blocks)


def next_chunks(chunks, narrow, order, prepared):
    _, width = prepared[-1].shape
    block = prepared[0].shape[1]
    groups = width // block
    parts = chunk_shapes(chunks, narrow, groups, block)
    return pl.pallas_call(
        functools.partial(next_kernel, chunks),
        out_shape=tuple(parts),
        in_specs=[BULK] + [VECTORS] * 5,
        out_specs=(VECTORS,) * len(parts),
        scratch_shapes=[*chunk_scratch(chunks, narrow, order, groups, block), pltpu.SemaphoreType.DMA],
        compiler_params=pltpu.CompilerParams(vmem_limit_bytes=24 << 20),
    )(order, *prepared)


def pick_kernel(keep, swapped, *outs):
    wide, narrow = lax.axis_size("wide"), lax.axis_size("narrow")
    half = narrow // 2
    side = lax.axis_index("wide") // (wide // 2)
    high = lax.axis_index("narrow") // half
    for step, out in enumerate(outs):
        stay = (high ^ (step // half)) == side

        @pl.when(stay)
        def _(out=out, step=step):
            out[...] = keep[step % half]

        @pl.when(jnp.logical_not(stay))
        def _(out=out, step=step):
            out[...] = swapped[step % half]


def pick_chunk(keep, swapped, steps):
    return pl.pallas_call(
        pick_kernel,
        out_shape=(pltpu.VMEM(keep.shape[1:], F32),) * steps,
        in_specs=[VECTORS] * 2,
        out_specs=(VECTORS,) * steps,
        compiler_params=pltpu.CompilerParams(vmem_limit_bytes=2 << 20),
    )(keep, swapped)


def place_kernel(low0, count, *refs):
    steps = lax.axis_size("narrow")
    pieces, result, sems = refs[:steps], refs[-2], refs[-1]
    place = lax.axis_index("narrow")
    copies = []
    for step in range(steps):
        copy = pltpu.make_async_copy(pieces[step], result.at[place ^ step, pl.ds(low0, count)], sems.at[step])
        copy.start()
        copies.append(copy)
    for copy in copies:
        copy.wait()


def place_chunk(chunk, pieces, shape, result):
    low0, count = chunk
    extra = [] if result is None else [result]
    return pl.pallas_call(
        functools.partial(place_kernel, low0, count),
        out_shape=jax.ShapeDtypeStruct(shape, F32),
        in_specs=[VECTORS] * len(pieces) + [BULK] * len(extra),
        out_specs=BULK,
        scratch_shapes=[pltpu.SemaphoreType.DMA((len(pieces),))],
        input_output_aliases={len(pieces): 0} if extra else {},
        compiler_params=pltpu.CompilerParams(vmem_limit_bytes=2 << 20),
    )(*pieces, *extra)


def local(state, col_blocks, row_blocks, col_pattern, row_pattern, qubit_order):
    rows, slabs, width = state.shape
    block = row_blocks.shape[-1]
    groups = slabs * width // block
    wide, narrow = lax.axis_size("wide"), lax.axis_size("narrow")
    top = wide // 2
    half = narrow // 2
    per_piece = rows // narrow
    unit = per_piece // sum(SHARES)
    wide_pairs = [(w, w ^ top) for w in range(wide)]
    counts = [share * unit for share in SHARES]
    chunks = [(sum(counts[:j]), count) for j, count in enumerate(counts)]
    parts = []
    made = first_chunks(
        chunks[:FIRST], narrow, state.reshape(rows, groups, block), row_blocks[0], col_blocks[0],
        row_pattern, col_pattern, qubit_order)
    sides = list(made[: 2 * FIRST])
    prepared = made[len(sides) :]
    for j, chunk in enumerate(chunks):
        _, count = chunk
        if j >= FIRST:
            sides += next_chunks((chunk,), narrow, qubit_order, prepared)
        keep, send = sides.pop(0), sides.pop(0)
        shape = (half, count, groups, block)
        swapped = lax.ppermute(send.reshape(shape), "wide", wide_pairs)
        picked = pick_chunk(keep.reshape(shape), swapped, narrow)
        moved = [picked[0]]
        for step in range(1, narrow):
            moved.append(lax.ppermute(picked[step], "narrow", [(n, n ^ step) for n in range(narrow)]))
        parts.append(tuple(moved))
    result = None
    for j, chunk in enumerate(chunks):
        result = place_chunk(chunk, parts[j], (narrow, per_piece, groups, block), result)
    return result.reshape(state.shape)


def solution(mesh):
    return jax.shard_map(
        local,
        mesh=mesh,
        in_specs=(P(("wide", "narrow"), None, None), P(), P(), P(), P(), P()),
        out_specs=P(("wide", "narrow"), None, None),
        check_vma=False,
    )
```
